32 devices in a mesh: seq: 8 (over y, x, core), exp: 4 (over z).
Axes of the slice: x: 2, y: 2, z: 4, core: 2. Of those that a mesh axis runs over, the one named last changes fastest.
Arguments:
- tokens: bfloat16 [4, 256, 2048], P('exp', 'seq'), may hold values from -6 to 6
- grad_out: bfloat16 [4, 256, 2048], P('exp', 'seq'), may hold values from -6 to 6
- expert_ids: int32 [4, 256, 8], P('exp', 'seq'), may hold values from 0 to 31, all different within a row; in each aligned block of 256 rows (0 to 255, 256 to 511, ..., all dimensions but the last counted through in order) at most 128 rows name the same one
- gate_probs: bfloat16 [4, 256, 8], P('exp', 'seq'), may hold values from 0.049804688 to 0.34960938
- w_gate: bfloat16 [32, 2048, 768], P(('seq', 'exp')), may hold values from -0.125 to 0.125
- w_up: bfloat16 [32, 2048, 768], P(('seq', 'exp')), may hold values from -0.125 to 0.125
- w_down: bfloat16 [32, 768, 2048], P(('seq', 'exp')), may hold values from -0.21875 to 0.21875
Outputs:
- layer_out: bfloat16 [4, 256, 2048], P('exp', 'seq')
- grad_tokens: bfloat16 [4, 256, 2048], P('exp', 'seq')
- grad_probs: float32 [4, 256, 8], P('exp', 'seq')
- grad_gate: bfloat16 [32, 2048, 768], P(('seq', 'exp'))
- grad_up: bfloat16 [32, 2048, 768], P(('seq', 'exp'))
- grad_down: bfloat16 [32, 768, 2048], P(('seq', 'exp'))
The draws below stay inside these ranges and needn't reach their ends.
Inputs may be any that keep to these rules, and one draw needn't show every extreme that they name: `expert_ids`: within one group of 256 tokens no expert is named by more than 128 of them, and in some group some expert is named by exactly 128; a token names 8 different experts.
All inputs are finite; a program needn't handle non-finite values.
Results may differ from the reference program's by a relative error of at most 0.0064.
Values may be sent and summed in bfloat16 or wider, within the bound.
No kernel may reach another device: no remote copies, remote signals or barrier semaphores. Data moves between devices by JAX's collectives and lax.ppermute only.
A program may use at most 128 MiB of HBM per device.

```python
import math
import jax
import jax.numpy as jnp
import numpy as np
from jax import lax

D = 2048
FF = 768
TOP = 8
EXPERTS = 32
GROUPS = 4
GROUP_TOK = 256
CAP = 128


def block_scale(key, dims, pieces, smallest, top_value):
    def one(position, shards_of):
        heights = jax.random.uniform(jax.random.fold_in(jax.random.fold_in(key, 6), position), (shards_of,), jnp.float32, smallest / len(pieces), top_value / len(pieces))
        return jnp.repeat(jnp.exp(heights), dims[position] // shards_of).reshape((-1,) + (1,) * (len(dims) - position - 1))

    factor_of = one(*pieces[0])
    for cut in pieces[1:]:
        factor_of = factor_of * one(*cut)
    return factor_of


def assign_block(key, own, number, rows, amount, top, reach, lean):
    sequence = jax.random.permutation(key, amount)
    crowded, ordinary = load_shares(amount, rows * top, reach, lean, True), load_shares(amount, rows * top, reach, lean, False)
    places = jnp.arange(amount)

    def named(sizes, turn):
        used = int((sizes > 0).sum())
        fixed = max(1, used // 4)
        shifted = fixed + (places - fixed + turn * (used - fixed)) % max(1, amount - fixed)
        return jnp.zeros((amount,), jnp.int32).at[sequence[jnp.where(places < fixed, places, shifted)]].set(jnp.asarray(sizes, jnp.int32))

    sizes = jnp.where(number % 4 == 0, named(crowded, number // 4), named(ordinary, number - number // 4 - 1))
    mixed = jax.random.permutation(jax.random.fold_in(own, 3), amount)
    source_of, receiver = mixed[0:amount // 2 * 2:2], mixed[1:amount // 2 * 2:2]
    slack = jnp.minimum(sizes[source_of] - 1, reach - sizes[receiver]) // 2
    slack = jnp.where((source_of == sequence[0]) | (receiver == sequence[0]) | (sizes[receiver] == 0), 0, jnp.maximum(slack, 0))
    shifted = jax.random.randint(jax.random.fold_in(own, 4), (amount // 2,), 0, 1 << 20) % (slack + 1)
    sizes = sizes.at[source_of].add(-shifted).at[receiver].add(shifted)
    members = jnp.searchsorted(jnp.cumsum(sizes), jnp.arange(rows * top), side="right").astype(jnp.int32)
    table = members.reshape(top, rows).T
    table = table[jax.random.permutation(jax.random.fold_in(own, 1), rows)]
    turn = jax.random.randint(jax.random.fold_in(own, 2), (rows, 1), 0, top)
    return jnp.take_along_axis(table, (jnp.arange(top)[None, :] + turn) % top, axis=1)


def load_shares(count, total, most, slope, full):
    portions = [(1 << 20) // math.isqrt(rank ** slope) + 1 for rank in range(1, count + 1)]
    largest = most if full else min(most, max(-(-total // count), total * portions[0] // sum(portions)))
    least = 1 if total - largest >= count - 1 else 0
    counts, spare = [largest] + [least] * (count - 1), total - largest - least * (count - 1)
    while spare > 0:
        candidates = [i for i in range(1, count) if counts[i] < largest] or [i for i in range(1, count) if counts[i] < most]
        whole, remaining = sum([portions[i] for i in candidates]), spare
        for i in candidates:
            more = min(most - counts[i], max(1, remaining * portions[i] // whole), spare)
            counts[i] = counts[i] + more
            spare = spare - more
    return np.array(counts)


def normal_values(rng, dims, deviation, most, cuts=(), held_as=jnp.bfloat16):
    entries = deviation * jax.random.normal(rng, dims, jnp.float32)
    if cuts:
        entries = entries * block_scale(rng, dims, cuts, -0.22, 0.18)
    return jnp.clip(entries, -most, most).astype(held_as)


def setup_inputs(seed: int = 0) -> dict:
    arg_keys = jax.random.split(jax.random.key(seed), 8)
    tokens = normal_values(arg_keys[0], (GROUPS, GROUP_TOK, D), 1.0, 6.0, ((0, 4), (1, 8)))
    grad_out = normal_values(arg_keys[1], (GROUPS, GROUP_TOK, D), 1.0, 6.0, ((0, 4), (1, 8)))
    expert_ids_keys = jax.random.split(jax.random.fold_in(arg_keys[2], 1), GROUPS * GROUP_TOK // GROUP_TOK)
    expert_ids_turns = jax.random.permutation(jax.random.fold_in(arg_keys[2], 3), GROUPS * GROUP_TOK // GROUP_TOK)
    expert_ids = jax.vmap(lambda own, number: assign_block(jax.random.fold_in(arg_keys[2], 2), own, number, GROUP_TOK, EXPERTS, TOP, CAP, 2))(expert_ids_keys, expert_ids_turns).reshape((GROUPS, GROUP_TOK, TOP))
    gate_probs = jnp.clip(0.049804688 + 0.2998047 * jax.random.uniform(arg_keys[3], (GROUPS, GROUP_TOK, TOP), jnp.float32) ** block_scale(arg_keys[3], (GROUPS, GROUP_TOK, TOP), ((0, 4), (1, 8)), -0.2, 0.2), 0.049804688, 0.34960938).astype(jnp.bfloat16)
    w_gate = normal_values(arg_keys[4], (EXPERTS, D, FF), D ** -0.5, 0.125, ((0, 32),))
    w_up = normal_values(arg_keys[5], (EXPERTS, D, FF), D ** -0.5, 0.125, ((0, 32),))
    w_down = normal_values(arg_keys[6], (EXPERTS, FF, D), FF ** -0.5, 0.21875, ((0, 32),))
    return dict(tokens=tokens, grad_out=grad_out, expert_ids=expert_ids, gate_probs=gate_probs, w_gate=w_gate, w_up=w_up, w_down=w_down)


def reference(tokens, grad_out, expert_ids, gate_probs, w_gate, w_up, w_down):
    inputs = tokens.reshape(-1, D)
    cotangent = grad_out.reshape(-1, D)
    assigned = expert_ids.reshape(-1).astype(jnp.int32)
    weights = gate_probs.reshape(-1).astype(jnp.float32)
    count_all = assigned.shape[0]
    most_load = GROUPS * CAP
    order = jnp.argsort(assigned, stable=True).astype(jnp.int32)
    loads = jnp.bincount(assigned, length=EXPERTS).astype(jnp.int32)
    starts = (jnp.cumsum(loads) - loads).astype(jnp.int32)
    slot_range = jnp.arange(most_load, dtype=jnp.int32)

    def expert_step(carry, expert):
        out_all, grad_all = carry
        filled = slot_range < loads[expert]
        where_from = jnp.minimum(starts[expert] + slot_range, count_all - 1).astype(jnp.int32)
        holder = jnp.where(filled, order[where_from], count_all).astype(jnp.int32)
        safe = jnp.where(filled, holder, 0).astype(jnp.int32)
        token_of = (safe // TOP).astype(jnp.int32)
        rows_in = jnp.where(filled[:, None], inputs[token_of], jnp.zeros((), inputs.dtype))
        gate_pre = jnp.dot(rows_in, w_gate[expert], preferred_element_type=jnp.float32)
        up_pre = jnp.dot(rows_in, w_up[expert], preferred_element_type=jnp.float32)
        sigma = jax.nn.sigmoid(gate_pre)
        active = gate_pre * sigma
        hidden = (active * up_pre).astype(jnp.bfloat16)
        expert_out = jnp.dot(hidden, w_down[expert], preferred_element_type=jnp.float32).astype(jnp.bfloat16)
        slot_gate = jnp.where(filled, weights[safe], jnp.float32(0.0))
        d_out = (slot_gate[:, None] * cotangent[token_of].astype(jnp.float32)).astype(jnp.bfloat16)
        d_hidden = lax.dot_general(d_out, w_down[expert], (((1,), (1,)), ((), ())), preferred_element_type=jnp.float32)
        grad_down = lax.dot_general(hidden, d_out, (((0,), (0,)), ((), ())), preferred_element_type=jnp.float32).astype(jnp.bfloat16)
        d_gate_pre = (d_hidden * up_pre * sigma * (1.0 + gate_pre * (1.0 - sigma))).astype(jnp.bfloat16)
        d_up_pre = (d_hidden * active).astype(jnp.bfloat16)
        grad_gate = lax.dot_general(rows_in, d_gate_pre, (((0,), (0,)), ((), ())), preferred_element_type=jnp.float32).astype(jnp.bfloat16)
        grad_up = lax.dot_general(rows_in, d_up_pre, (((0,), (0,)), ((), ())), preferred_element_type=jnp.float32).astype(jnp.bfloat16)
        d_rows = lax.dot_general(d_gate_pre, w_gate[expert], (((1,), (1,)), ((), ())), preferred_element_type=jnp.float32)
        d_rows = d_rows + lax.dot_general(d_up_pre, w_up[expert], (((1,), (1,)), ((), ())), preferred_element_type=jnp.float32)
        d_rows = d_rows.astype(jnp.bfloat16)
        out_all = out_all.at[holder].set(expert_out, mode="drop")
        grad_all = grad_all.at[holder].set(d_rows, mode="drop")
        return (out_all, grad_all), (grad_gate, grad_up, grad_down)

    start_out = jnp.zeros((count_all, D), jnp.bfloat16)
    start_grad = jnp.zeros((count_all, D), jnp.bfloat16)
    (out_all, grad_all), (grad_gate, grad_up, grad_down) = lax.scan(
        expert_step, (start_out, start_grad), jnp.arange(EXPERTS, dtype=jnp.int32))
    token_count = inputs.shape[0]
    out_three = out_all.reshape(token_count, TOP, D).astype(jnp.float32)
    weight_three = weights.reshape(token_count, TOP)
    layer_out = jnp.sum(weight_three[:, :, None] * out_three, axis=1).astype(jnp.bfloat16)
    grad_probs = jnp.sum(cotangent.astype(jnp.float32)[:, None, :] * out_three, axis=2)
    grad_tokens = jnp.sum(grad_all.reshape(token_count, TOP, D).astype(jnp.float32), axis=1).astype(jnp.bfloat16)
    return (layer_out.reshape(GROUPS, GROUP_TOK, D),
            grad_tokens.reshape(GROUPS, GROUP_TOK, D),
            grad_probs.reshape(GROUPS, GROUP_TOK, TOP),
            grad_gate, grad_up, grad_down)
```

```python
import jax
import jax.numpy as jnp
from jax import lax
from jax.experimental import pallas as pl
from jax.experimental.pallas import tpu as pltpu
from jax.sharding import PartitionSpec as P


F32 = jnp.float32
BF16 = jnp.bfloat16
LANES = 128
HBM = pl.BlockSpec(memory_space=pl.ANY)
SMEM = pl.BlockSpec(memory_space=pltpu.SMEM)


def dot(a, b, ca=1, cb=0):
    return lax.dot_general(a, b, (((ca,), (cb,)), ((), ())), preferred_element_type=F32)


class Copies:
    def __init__(self, sems):
        self.sems, self.used = sems, 0

    def start(self, src, dst):
        copy = pltpu.make_async_copy(src, dst, self.sems.at[self.used])
        self.used += 1
        copy.start()
        return copy


def tiles(size, tile):
    return [slice(at, at + tile) for at in range(0, size, tile)]


def load_pieces(copies, refs, places, held):
    width = refs[0].shape[-1]
    return [
        copies.start(ref, held.at[pl.ds(g0, gn), pl.ds(b0, bn), :, pl.ds(0, width)])
        for ref, (g0, gn, b0, bn) in zip(refs, places)
    ]


def forward_kernel(cfg, e_ref, *refs):
    groups, cap, top, places, splits = cfg
    n = len(places)
    pieces, (wg, wu, wd) = refs[:n], refs[n : n + 3]
    outs = refs[n + 3 : n + 11 + len(splits)]
    rows_o, act_o, slope_o, hid_o, out_o, pick_o, gate_o, ids_o = outs[:8]
    parts = outs[8:]
    held, vg, vu, vd, rows, act, slope, hid, out, pick, wpick, gate, ids, sems = refs[n + 11 + len(splits) :]
    d, ff = wg.shape
    tok = held.shape[1] * held.shape[2]
    expert = e_ref[0].astype(F32)
    copies = Copies(sems)
    xs = load_pieces(copies, pieces, places, held)
    ws = []
    for t in tiles(ff, 256):
        ws.append((copies.start(wg.at[:, t], vg.at[:, t]), copies.start(wu.at[:, t], vu.at[:, t])))
    wds = copies.start(wd, vd)
    before = (
        lax.broadcasted_iota(jnp.int32, (tok, tok), 0) > lax.broadcasted_iota(jnp.int32, (tok, tok), 1)
    ).astype(F32).astype(BF16)
    slot = lax.broadcasted_iota(jnp.int32, (tok, cap), 1).astype(F32)
    for x in xs:
        x.wait()
    sends = []

    def chosen(extra):
        lane = lax.broadcasted_iota(jnp.int32, extra.shape, 1)
        hit = (extra == expert) & (lane < top)
        weight = jnp.where(hit, pltpu.roll(extra, LANES - 2 * top, 1), 0.0)
        return jnp.sum(jnp.where(hit, 1.0, 0.0), 1, keepdims=True), jnp.sum(weight, 1, keepdims=True)

    for g in range(groups):
        of = slice(g * cap, (g + 1) * cap)
        ts = slice(g * tok, (g + 1) * tok)
        extra = held[g, :, :, d:].reshape(tok, LANES)
        ids[ts] = extra
        member, weight = chosen(extra.astype(F32))
        member = jnp.broadcast_to(member, (tok, cap))
        position = dot(before, member.astype(BF16))
        one = jnp.where((position == slot) & (member > 0.5), 1.0, 0.0)
        pick[ts] = one.astype(BF16)
        wpick[ts] = (one * weight).astype(BF16)
        got = dot(pick[ts], held[g].reshape(tok, d + LANES), 0, 0)
        rows[of] = got[:, :d].astype(BF16)
        gate[of] = jnp.broadcast_to(chosen(got[:, d:])[1], (cap, LANES))
    sends += [copies.start(a, b) for a, b in ((rows, rows_o), (pick, pick_o), (gate, gate_o), (ids, ids_o))]
    for t, pair in zip(tiles(ff, 256), ws):
        for copy in pair:
            copy.wait()
        pre = dot(rows[...], vg[:, t])
        up = dot(rows[...], vu[:, t])
        sigma = jax.nn.sigmoid(pre)
        active = pre * sigma
        act[:, t] = active
        slope[:, t] = up * sigma * (1.0 + pre * (1.0 - sigma))
        hid[:, t] = (active * up).astype(BF16)
    sends += [copies.start(a, b) for a, b in ((act, act_o), (slope, slope_o), (hid, hid_o))]
    wds.wait()
    for t in tiles(d, 512):
        out[:, t] = dot(hid[...], vd[:, t]).astype(BF16)
        for g in range(groups):
            spread = dot(wpick[g * tok : (g + 1) * tok], out[g * cap : (g + 1) * cap, t])
            held[g, :, :, t] = spread.astype(BF16).reshape(held.shape[1], held.shape[2], 512)
        for part, (b0, bn) in zip(parts, splits):
            sends.append(copies.start(held.at[:, pl.ds(b0, bn), :, t], part.at[:, :, :, t]))
    sends.append(copies.start(out, out_o))
    for s in sends:
        s.wait()


def backward_kernel(cfg, e_ref, *refs):
    groups, cap, top, places, splits = cfg
    n = len(places)
    pieces = refs[:n]
    wg, wu, wd, act_i, slope_i, out_i, pick_i, gate_i, ids_i = refs[n : n + 9]
    outs = refs[n + 9 : n + 12 + len(splits)]
    dout_o, dgate_o, dup_o = outs[:3]
    parts = outs[3:]
    held, vg, vu, vd, act, slope, out, pick, gate, ids, dout, dgate, dup, sems = refs[n + 12 + len(splits) :]
    d, ff = wg.shape
    tok = held.shape[1] * held.shape[2]
    expert = e_ref[0].astype(F32)
    copies = Copies(sems)
    small = [copies.start(a, b) for a, b in ((pick_i, pick), (gate_i, gate), (ids_i, ids), (out_i, out))]
    small += load_pieces(copies, pieces, places, held)
    wds = copies.start(wd, vd)
    acts = [copies.start(act_i, act), copies.start(slope_i, slope)]
    ws = [copies.start(wg, vg), copies.start(wu, vu)]
    for copy in small:
        copy.wait()
    sends = []
    lane = lax.broadcasted_iota(jnp.int32, (cap, LANES), 1)
    for g in range(groups):
        of = slice(g * cap, (g + 1) * cap)
        ts = slice(g * tok, (g + 1) * tok)
        got = dot(pick[ts], held[g, :, :, :d].reshape(tok, d), 0, 0)
        dout[of] = (gate[of, :1] * got).astype(BF16)
        score = jnp.sum(got * out[of].astype(F32), 1, keepdims=True)
        high = score.astype(BF16).astype(F32)
        both = jnp.where(lane < top, high, jnp.where(lane < 2 * top, score - high, 0.0))
        spread = dot(pick[ts], both.astype(BF16))
        spread = jnp.where(ids[ts].astype(F32) == expert, spread, 0.0)
        held[g, :, :, d:] = spread.astype(BF16).reshape(held.shape[1], held.shape[2], LANES)
    sends.append(copies.start(dout, dout_o))
    wds.wait()
    for copy in acts:
        copy.wait()
    for t in tiles(ff, 256):
        dhid = dot(dout[...], vd[t, :], 1, 1)
        dgate[:, t] = (dhid * slope[:, t]).astype(BF16)
        dup[:, t] = (dhid * act[:, t]).astype(BF16)
    sends += [copies.start(dgate, dgate_o), copies.start(dup, dup_o)]
    for copy in ws:
        copy.wait()
    for i, t in enumerate(tiles(d, 512)):
        drow = (dot(dgate[...], vg[t, :], 1, 1) + dot(dup[...], vu[t, :], 1, 1)).astype(BF16)
        for g in range(groups):
            spread = dot(pick[g * tok : (g + 1) * tok], drow[g * cap : (g + 1) * cap])
            held[g, :, :, t] = spread.astype(BF16).reshape(held.shape[1], held.shape[2], 512)
        u = slice(t.start, d + LANES) if t.stop == d else t
        for part, (b0, bn) in zip(parts, splits):
            sends.append(copies.start(held.at[:, pl.ds(b0, bn), :, u], part.at[:, :, :, u]))
    for s in sends:
        s.wait()


def swap(x, axis, bit):
    return lax.ppermute(x, axis, [(i, i ^ bit) for i in range(lax.axis_size(axis))])


def short(x):
    return x.astype(BF16)


def wide(x):
    return x.astype(F32)


def gather_all(x, fast):
    if not fast:
        whole = lax.all_gather(lax.all_gather(x[None], "seq", axis=0), "exp", axis=0)
        groups, blocks = lax.axis_size("exp"), lax.axis_size("seq")
        return [whole.reshape(groups, blocks, *x.shape)], [(0, groups, 0, blocks)]
    own = jnp.stack([x] + [swap(x, "exp", k) for k in (1, 2, 3)])
    beside = swap(own, "seq", 2)
    above = swap(own, "seq", 4)
    far_a = swap(beside[:2], "seq", 4)
    far_b = swap(above[2:], "seq", 2)
    pieces = [own, beside, above, far_a, far_b]
    places = [(0, 4, 0, 1), (0, 4, 1, 1), (0, 4, 2, 1), (0, 2, 3, 1), (2, 2, 3, 1)]
    pieces = [p[:, None] for p in pieces]
    others = [swap(p, "seq", 1) for p in pieces]
    return pieces + others, places + [(a, b, c + 4, e) for a, b, c, e in places]


def scatter_sum(parts, fast):
    if not fast:
        total = lax.psum_scatter(parts[0], "exp", scatter_dimension=0, tiled=True)
        return wide(lax.psum_scatter(total, "seq", scatter_dimension=1, tiled=True)[0, 0])
    mine, other = parts
    came = swap(other, "seq", 1)

    def both(i, a=0, b=4):
        return wide(mine[a:b, i]) + wide(came[a:b, i])

    far = [short(both(3, 0, 2)), short(both(3, 2, 4))]
    to_above = swap(far[0], "seq", 4)
    to_beside = swap(far[1], "seq", 2)
    beside = jnp.concatenate([short(both(1, 0, 2) + wide(to_above)), short(both(1, 2, 4))])
    above = jnp.concatenate([short(both(2, 0, 2)), short(both(2, 2, 4) + wide(to_beside))])
    beside = swap(beside, "seq", 2)
    above = swap(above, "seq", 4)

    def plane(z):
        return both(0, z, z + 1)[0] + wide(beside[z]) + wide(above[z])

    total = plane(0)
    for z in (1, 2, 3):
        total = total + wide(swap(short(plane(z)), "exp", z))
    return total


def on_device(tokens, grad_out, expert_ids, gate_probs, w_gate, w_up, w_down):
    groups = lax.axis_size("exp")
    n_seq = lax.axis_size("seq")
    fast = groups == 4 and n_seq == 8
    _, tok_dev, d = tokens.shape
    ff = w_gate.shape[2]
    top = expert_ids.shape[2]
    tok = tok_dev * n_seq
    cap = 2 * tok_dev * top // groups
    slots = groups * cap
    expert = (lax.axis_index("seq") * groups + lax.axis_index("exp")).astype(jnp.int32).reshape(1)
    ids = expert_ids[0].astype(BF16)
    blank = jnp.zeros((tok_dev, LANES - 3 * top), BF16)
    xs, places = gather_all(jnp.concatenate([tokens[0], ids, ids, gate_probs[0], blank], 1), fast)
    gs, _ = gather_all(grad_out[0], fast)
    splits = ((0, 4), (4, 4)) if fast else ((0, n_seq),)
    cfg = (groups, cap, top, tuple(places), splits)
    vm = pltpu.VMEM
    sd = jax.ShapeDtypeStruct
    params = pltpu.CompilerParams(vmem_limit_bytes=60 * 2**20)
    weights = [vm((d, ff), BF16), vm((d, ff), BF16), vm((ff, d), BF16)]
    keep = [
        vm((slots, d), BF16), vm((slots, ff), F32), vm((slots, ff), F32), vm((slots, ff), BF16),
        vm((slots, d), BF16), vm((groups * tok, cap), BF16),
    ]
    late = [vm((slots, LANES), F32), vm((groups * tok, LANES), BF16)]

    def shapes(scratch):
        return [sd(s.shape, s.dtype) for s in scratch]

    def parts(width):
        return [sd((groups, bn, tok_dev, width), BF16) for _, bn in splits]

    fwd_out = shapes(keep) + shapes(late) + parts(d)
    rows, act, slope, hid, out, pick, gate, extra, *out_parts = pl.pallas_call(
        lambda *refs: forward_kernel(cfg, *refs),
        out_shape=fwd_out,
        in_specs=[SMEM] + [HBM] * (len(xs) + 3),
        out_specs=[HBM] * len(fwd_out),
        scratch_shapes=[vm((groups, n_seq, tok_dev, d + LANES), BF16)] + weights + keep
        + [vm((groups * tok, cap), BF16)] + late + [pltpu.SemaphoreType.DMA((64,))],
        compiler_params=params,
        name="forward",
    )(expert, *xs, w_gate[0], w_up[0], w_down[0])
    out_sum = scatter_sum(out_parts, fast)
    grads = [vm((slots, d), BF16), vm((slots, ff), BF16), vm((slots, ff), BF16)]
    bwd_out = shapes(grads) + parts(d + LANES)
    dout, dgate, dup, *row_parts = pl.pallas_call(
        lambda *refs: backward_kernel(cfg, *refs),
        out_shape=bwd_out,
        in_specs=[SMEM] + [HBM] * (len(gs) + 9),
        out_specs=[HBM] * len(bwd_out),
        scratch_shapes=[vm((groups, n_seq, tok_dev, d + LANES), BF16)] + weights + keep[1:3] + keep[4:6]
        + late + grads + [pltpu.SemaphoreType.DMA((64,))],
        compiler_params=params,
        name="backward",
    )(expert, *gs, w_gate[0], w_up[0], w_down[0], act, slope, out, pick, gate, extra)
    grad_gate = dot(rows, dgate, 0, 0).astype(BF16)
    grad_up = dot(rows, dup, 0, 0).astype(BF16)
    grad_down = dot(hid, dout, 0, 0).astype(BF16)
    row_sum = scatter_sum(row_parts, fast)
    probs = row_sum[:, d : d + top] + row_sum[:, d + top : d + 2 * top]
    return (
        short(out_sum)[None],
        short(row_sum[:, :d])[None],
        probs[None],
        grad_gate[None],
        grad_up[None],
        grad_down[None],
    )


def solution(mesh):
    tok = P("exp", "seq", None)
    exp = P(("seq", "exp"), None, None)
    return jax.shard_map(
        on_device,
        mesh=mesh,
        in_specs=(tok, tok, tok, tok, exp, exp, exp),
        out_specs=(tok, tok, tok, exp, exp, exp),
        check_vma=False,
    )
```
